32 devices in a mesh: groups: 2 (over x), row: 16 (over z, y, core).
Axes of the slice: x: 2, y: 2, z: 4, core: 2. Of those that a mesh axis runs over, the one named last changes fastest.
Arguments:
- design_matrix: bfloat16 [1024, 65536], P('groups', 'row'), parts along dimension 0, may hold values from -0.0546875 to 0.0546875
- targets: float32 [1024, 128], P(('groups', 'row')), parts along dimension 0, may hold values from -24 to 24
- linear: float32 [131072, 128], P(('groups', 'row')), parts along dimension 0, may hold values from -24 to 24
- diagonal: float32 [131072], P(('groups', 'row')), parts along dimension 0, may hold values from 0.1 to 2
- lower_code: int32 [131072, 128], P(('groups', 'row')), parts along dimension 0, may hold values from -192 to -17
- upper_code: int32 [131072, 128], P(('groups', 'row')), parts along dimension 0, may hold values from 16 to 191
Outputs:
- box_iterate: float32 [131072, 128], P(('groups', 'row')), parts along dimension 0
- scaled_dual: float32 [131072, 128], P(('groups', 'row')), parts along dimension 0
The draws below stay inside these ranges and needn't reach their ends.
There are 2 independent parts, one for each index of `groups`. The reference program is written for one: setup_inputs(seed, part) draws one part's arguments, and reference() takes and returns one part's arrays. A program takes and returns all parts, laid end to end along the dimension named above; each array names one. Nothing has to cross between parts.
All inputs are finite; a program needn't handle non-finite values.
Results may differ from the reference program's by a relative error of at most 0.00033.
Values may be sent and summed in bfloat16 or wider, within the bound.
No kernel may reach another device: no remote copies, remote signals or barrier semaphores. Data moves between devices by JAX's collectives and lax.ppermute only.
A program may use at most 128 MiB of HBM per device.

```python
import math
import jax
import jax.numpy as jnp
from jax import lax

N = 65536
K = 512
S = 128
ITERS = 4
DEPTH = 5


def place_ends(drawn, own_key, least, largest):
    longest = drawn.shape.index(max(drawn.shape))
    spots = []
    for shift in (0, 1):
        where = [jax.random.randint(jax.random.fold_in(own_key, axis), (), 0, length) for axis, length in enumerate(drawn.shape)]
        where[longest] = (where[longest] + shift) % drawn.shape[longest]
        spots.append(tuple(where))
    return drawn.at[spots[0]].set(least).at[spots[1]].set(largest)


def raised(array, key, source, target, shards_of, factor):
    def block_of(position):
        return (jnp.arange(array.shape[position]) // (array.shape[position] // shards_of)).reshape((-1,) + (1,) * (array.ndim - 1 - position))

    near = jax.random.permutation(key, shards_of)[block_of(target)]
    far = (block_of(target) + shards_of // 2) % shards_of
    return jnp.where((block_of(source) == near) | (block_of(source) == far), factor * array, array)


def level_of(key, extent, pieces, smallest, largest):
    loudness = 1.0
    for dim, shards_of in pieces:
        draws = jax.random.uniform(jax.random.fold_in(jax.random.fold_in(key, 6), dim), (shards_of,), jnp.float32, smallest / len(pieces), largest / len(pieces))
        loudness = loudness * jnp.repeat(jnp.exp(draws), extent[dim] // shards_of).reshape((-1,) + (1,) * (len(extent) - 1 - dim))
    return loudness


def gaussian(rng, extent, deviation, bound, shards=(), kind=jnp.bfloat16):
    values = jax.random.normal(rng, extent, jnp.float32) * deviation
    if len(shards) > 0:
        values = level_of(rng, extent, shards, -0.22, 0.18) * values
    return jnp.clip(values, min=-bound, max=bound).astype(kind)


def noise_with(own_key, extent, spread, reach, shards, heavy, held_as=jnp.bfloat16):
    values = spread * jax.random.normal(own_key, extent, jnp.float32)
    if shards:
        values = values * level_of(own_key, extent, shards, -0.22, 0.18)
    return jnp.clip(raised(values, jax.random.fold_in(own_key, 3), *heavy), -reach, reach).astype(held_as)


def setup_inputs(seed: int = 0, part: int = 0) -> dict:
    key_of = jax.random.split(jax.random.key(seed), 7)
    part_keys = jax.random.split(jax.random.fold_in(key_of[6], part), 7)
    design_matrix = noise_with(part_keys[0], (K, N), (max(N // 3, 2 * K)) ** -0.5, 0.0546875, ((1, 16),), (1, 0, 16, 2.0))
    targets = gaussian(part_keys[1], (K, S), 4.0, 24.0, ((0, 16),), jnp.float32)
    linear = gaussian(part_keys[2], (N, S), 4.0, 24.0, ((0, 16),), jnp.float32)
    diagonal = jnp.clip(jnp.exp(math.log(2.0) - 2.9957323 * jax.random.uniform(part_keys[3], (N,), jnp.float32) ** level_of(part_keys[3], (N,), ((0, 16),), -0.2, 0.2)), 0.1, 2.0)
    lower_code = place_ends(jax.random.randint(part_keys[4], (N, S), -192, -16), jax.random.fold_in(part_keys[4], 1), -192, (-16) - 1).astype(jnp.int32)
    upper_code = place_ends(jax.random.randint(part_keys[5], (N, S), 16, 192), jax.random.fold_in(part_keys[5], 1), 16, 191).astype(jnp.int32)
    return {"design_matrix": design_matrix, "targets": targets, "linear": linear, "diagonal": diagonal, "lower_code": lower_code, "upper_code": upper_code}


rho_plus_lip = 7.0


def solve_small(matrix, rhs):
    count = len(rhs)
    table = [list(line) for line in matrix]
    right = list(rhs)
    for p in range(count):
        for i in range(p + 1, count):
            factor = table[i][p] / table[p][p]
            for j in range(p, count):
                table[i][j] = table[i][j] - factor * table[p][j]
            right[i] = right[i] - factor * right[p]
    result = [None] * count
    for i in reversed(range(count)):
        total = right[i]
        for j in range(i + 1, count):
            total = total - table[i][j] * result[j]
        result[i] = total / table[i][i]
    return result


def mix_weights(gram):
    count = len(gram)
    trace = gram[0][0]
    for i in range(1, count):
        trace = trace + gram[i][i]
    shift = 0.01 * trace / count + 1e-6
    matrix = [[gram[i][j] + (shift if i == j else 0.0) for j in range(count)] for i in range(count)]
    solved = solve_small(matrix, [jnp.ones_like(trace)] * count)
    total = solved[0]
    for i in range(1, count):
        total = total + solved[i]
    return [item / total for item in solved]


def reference(design_matrix, targets, linear, diagonal, lower_code, upper_code):
    lower = lower_code.astype(jnp.float32) / 64.0
    upper = upper_code.astype(jnp.float32) / 64.0
    step_size = (1.0 / (rho_plus_lip + diagonal))[:, None]

    def apply_map(state):
        point = state[0] - state[1]
        point_b = point.astype(jnp.bfloat16)
        product = jnp.dot(design_matrix, point_b, preferred_element_type=jnp.float32)
        misfit = (product - targets).astype(jnp.bfloat16)
        gradient = lax.dot_general(design_matrix, misfit, (((0,), (0,)), ((), ())), preferred_element_type=jnp.float32)
        gradient = gradient + diagonal[:, None] * point + linear
        moved = point - step_size * gradient
        boxed = jnp.clip(moved + state[1], lower, upper)
        scaled = state[1] + moved - boxed
        return jnp.stack([boxed, scaled])

    state = jnp.zeros((2,) + linear.shape, jnp.float32)
    hist_mapped = []
    hist_change = []
    for iteration in range(ITERS):
        mapped = apply_map(state)
        hist_mapped.append(mapped)
        hist_change.append(mapped - state)
        if len(hist_mapped) > DEPTH:
            hist_mapped.pop(0)
            hist_change.pop(0)
        stacked = jnp.stack(hist_change)
        whole = jnp.einsum('icns,jcns->ijs', stacked, stacked, precision=lax.Precision.HIGHEST)
        count = len(hist_change)
        gram = [[whole[i, j] for j in range(count)] for i in range(count)]
        alpha = mix_weights(gram)
        combined = alpha[0][None, None, :] * hist_mapped[0]
        for i in range(1, count):
            combined = combined + alpha[i][None, None, :] * hist_mapped[i]
        state = jnp.stack([jnp.clip(combined[0], lower, upper), combined[1]])
    return state[0], state[1]
```

```python
import jax
import jax.numpy as jnp
from jax import lax
from jax.sharding import PartitionSpec as P

ITERS = 4


rho_plus_lip = 7.0


def solve_small(matrix, rhs):
    count = len(rhs)
    table = [list(line) for line in matrix]
    right = list(rhs)
    for p in range(count):
        for i in range(p + 1, count):
            factor = table[i][p] / table[p][p]
            for j in range(p, count):
                table[i][j] = table[i][j] - factor * table[p][j]
            right[i] = right[i] - factor * right[p]
    result = [None] * count
    for i in reversed(range(count)):
        total = right[i]
        for j in range(i + 1, count):
            total = total - table[i][j] * result[j]
        result[i] = total / table[i][i]
    return result


def mix_weights(gram):
    count = len(gram)
    trace = gram[0][0]
    for i in range(1, count):
        trace = trace + gram[i][i]
    shift = 0.01 * trace / count + 1e-06
    matrix = [[gram[i][j] + (shift if i == j else 0.0) for j in range(count)] for i in range(count)]
    solved = solve_small(matrix, [jnp.ones_like(trace)] * count)
    total = solved[0]
    for i in range(1, count):
        total = total + solved[i]
    return [item / total for item in solved]


def apply_map(design_matrix, misfit, z, u, linear, diag, step_size, lower, upper):
    gradient = lax.dot_general(
        design_matrix,
        misfit,
        (((0,), (0,)), ((), ())),
        preferred_element_type=jnp.float32,
    )
    point = z - u
    gradient = gradient + diag * point + linear
    moved = point - step_size * gradient
    boxed = jnp.clip(moved + u, lower, upper)
    return boxed, u + moved - boxed


def per_device(design_matrix, targets, linear, diagonal, lower_code, upper_code):
    lower = lower_code.astype(jnp.float32) / 64.0
    upper = upper_code.astype(jnp.float32) / 64.0
    diag = diagonal[:, None]
    step_size = 1.0 / (rho_plus_lip + diag)
    z = jnp.zeros(linear.shape, jnp.float32)
    u = z
    mapped = []
    change = []
    gram = {}
    fresh = []
    for iteration in range(ITERS):
        if iteration == 0:
            misfit = (-targets).astype(jnp.bfloat16)
        else:
            product = lax.psum_scatter(
                jnp.dot(
                    design_matrix,
                    (z - u).astype(jnp.bfloat16),
                    preferred_element_type=jnp.float32,
                ),
                "row",
                scatter_dimension=0,
                tiled=True,
            )
            misfit = (product - targets).astype(jnp.bfloat16)
        misfit = lax.all_gather(misfit, "row", axis=0, tiled=True)
        boxed, scaled = apply_map(
            design_matrix, misfit, z, u, linear, diag, step_size, lower, upper
        )
        mapped.append((boxed, scaled))
        change.append((boxed - z, scaled - u))
        for i in range(iteration + 1):
            fresh.append(
                (
                    (i, iteration),
                    jnp.sum(
                        change[i][0] * change[iteration][0]
                        + change[i][1] * change[iteration][1],
                        axis=0,
                    ),
                )
            )
        if iteration == 0:
            z, u = boxed, scaled
            continue
        partial = jnp.stack([item for _, item in fresh])
        whole = jnp.sum(lax.all_gather(partial, "row", axis=0), axis=0)
        for k, (pair, _) in enumerate(fresh):
            gram[pair] = whole[k]
        fresh = []
        count = iteration + 1
        alpha = mix_weights(
            [
                [gram[(min(i, j), max(i, j))] for j in range(count)]
                for i in range(count)
            ]
        )
        z = alpha[0][None, :] * mapped[0][0]
        u = alpha[0][None, :] * mapped[0][1]
        for i in range(1, count):
            z = z + alpha[i][None, :] * mapped[i][0]
            u = u + alpha[i][None, :] * mapped[i][1]
        z = jnp.clip(z, lower, upper)
    return z, u


def solution(mesh):
    in_specs = (
        P("groups", "row"),
        P(("groups", "row"), None),
        P(("groups", "row"), None),
        P(("groups", "row")),
        P(("groups", "row"), None),
        P(("groups", "row"), None),
    )
    out_specs = (P(("groups", "row"), None), P(("groups", "row"), None))
    return jax.shard_map(
        per_device, mesh=mesh, in_specs=in_specs, out_specs=out_specs, check_vma=False
    )
```

```python
import jax
import jax.numpy as jnp
from jax import lax
from jax.sharding import PartitionSpec as P

ITERS = 4


rho_plus_lip = 7.0


def solve_small(matrix, rhs):
    count = len(rhs)
    table = [list(line) for line in matrix]
    right = list(rhs)
    for p in range(count):
        for i in range(p + 1, count):
            factor = table[i][p] / table[p][p]
            for j in range(p, count):
                table[i][j] = table[i][j] - factor * table[p][j]
            right[i] = right[i] - factor * right[p]
    result = [None] * count
    for i in reversed(range(count)):
        total = right[i]
        for j in range(i + 1, count):
            total = total - table[i][j] * result[j]
        result[i] = total / table[i][i]
    return result


def mix_weights(gram):
    count = len(gram)
    trace = gram[0][0]
    for i in range(1, count):
        trace = trace + gram[i][i]
    shift = 0.01 * trace / count + 1e-06
    matrix = [[gram[i][j] + (shift if i == j else 0.0) for j in range(count)] for i in range(count)]
    solved = solve_small(matrix, [jnp.ones_like(trace)] * count)
    total = solved[0]
    for i in range(1, count):
        total = total + solved[i]
    return [item / total for item in solved]


def sum_to_owner(part, count):
    rows = part.shape[0] // count
    return jnp.sum(
        lax.all_to_all(
            part.astype(jnp.bfloat16).reshape(count, rows, part.shape[1]),
            "row",
            0,
            0,
            tiled=True,
        ).astype(jnp.float32),
        axis=0,
    )


def to_everyone(part, count):
    got = lax.all_to_all(
        jnp.broadcast_to(part[None], (count,) + part.shape), "row", 0, 0, tiled=True
    )
    return got.reshape((count * part.shape[0],) + part.shape[1:])


def sum_everywhere(part, count):
    got = lax.all_to_all(
        jnp.broadcast_to(part[None], (count,) + part.shape), "row", 0, 0, tiled=True
    )
    return jnp.sum(got, axis=0)


def apply_map(design_matrix, misfit, z, u, linear, diag, step_size, lower, upper):
    gradient = lax.dot_general(
        design_matrix,
        misfit,
        (((0,), (0,)), ((), ())),
        preferred_element_type=jnp.float32,
    )
    point = z - u
    gradient = gradient + diag * point + linear
    moved = point - step_size * gradient
    boxed = jnp.clip(moved + u, lower, upper)
    return boxed, u + moved - boxed


def per_device(design_matrix, targets, linear, diagonal, lower_code, upper_code):
    lower = lower_code.astype(jnp.float32) / 64.0
    upper = upper_code.astype(jnp.float32) / 64.0
    diag = diagonal[:, None]
    step_size = 1.0 / (rho_plus_lip + diag)
    count_row = lax.axis_size("row")
    z = jnp.zeros(linear.shape, jnp.float32)
    u = z
    mapped = []
    change = []
    gram = {}
    fresh = []
    for iteration in range(ITERS):
        if iteration == 0:
            misfit = (-targets).astype(jnp.bfloat16)
        else:
            product = sum_to_owner(
                jnp.dot(
                    design_matrix,
                    (z - u).astype(jnp.bfloat16),
                    preferred_element_type=jnp.float32,
                ),
                count_row,
            )
            misfit = (product - targets).astype(jnp.bfloat16)
        misfit = to_everyone(misfit, count_row)
        boxed, scaled = apply_map(
            design_matrix, misfit, z, u, linear, diag, step_size, lower, upper
        )
        mapped.append((boxed, scaled))
        change.append((boxed - z, scaled - u))
        for i in range(iteration + 1):
            fresh.append(
                (
                    (i, iteration),
                    jnp.sum(
                        change[i][0] * change[iteration][0]
                        + change[i][1] * change[iteration][1],
                        axis=0,
                    ),
                )
            )
        if iteration == 0:
            z, u = boxed, scaled
            continue
        partial = jnp.stack([item for _, item in fresh])
        whole = sum_everywhere(partial, count_row)
        for k, (pair, _) in enumerate(fresh):
            gram[pair] = whole[k]
        fresh = []
        count = iteration + 1
        alpha = mix_weights(
            [
                [gram[(min(i, j), max(i, j))] for j in range(count)]
                for i in range(count)
            ]
        )
        z = alpha[0][None, :] * mapped[0][0]
        u = alpha[0][None, :] * mapped[0][1]
        for i in range(1, count):
            z = z + alpha[i][None, :] * mapped[i][0]
            u = u + alpha[i][None, :] * mapped[i][1]
        z = jnp.clip(z, lower, upper)
    return z, u


def solution(mesh):
    in_specs = (
        P("groups", "row"),
        P(("groups", "row"), None),
        P(("groups", "row"), None),
        P(("groups", "row")),
        P(("groups", "row"), None),
        P(("groups", "row"), None),
    )
    out_specs = (P(("groups", "row"), None), P(("groups", "row"), None))
    return jax.shard_map(
        per_device, mesh=mesh, in_specs=in_specs, out_specs=out_specs, check_vma=False
    )
```
